512 devices in a mesh: orb: 32 (over z, x_lo, core), spx: 16 (over x_hi, y).
Axes of the slice: x: 4 (x_hi: 2, x_lo: 2; x = x_hi * 2 + x_lo), y: 8, z: 8, core: 2. Of those that a mesh axis runs over, the one named last changes fastest.
Arguments:
- weights: float32 [131072], P('orb'), may hold values from 0.25 to 2
- losvd: bfloat16 [131072, 128, 64], P('orb', 'spx'), may hold values from 0 to 0.00390625
- occupancy: int32 [1024, 128], P('orb', 'spx'), may hold values 0 or 1
- template_of: int32 [131072], P('orb'), may hold values from 0 to 255
- templates: bfloat16 [256, 4160], P('orb'), may hold values from -0.046875 to 0.046875
- observed: float32 [128, 4096], P('spx'), may hold values from -6 to 6
- inv_sigma: float32 [128, 4096], P('spx'), may hold values from 0.5 to 2
Outputs:
- weights_next: float32 [131072], P('orb')
- residual: float32 [128, 4096], P('spx')
The draws below stay inside these ranges and needn't reach their ends.
All inputs are finite; a program needn't handle non-finite values. No bound on the sum of `occupancy` on one device may be relied on, other than what follows from the above.
Results may differ from the reference program's by a relative error of at most 0.0005.
Values may be sent and summed in bfloat16 or wider, within the bound.
No kernel may reach another device: no remote copies, remote signals or barrier semaphores. Data moves between devices by JAX's collectives and lax.ppermute only.
A program may use at most 64 MiB of HBM per device.

```python
import math
import jax
import jax.numpy as jnp
from jax import lax

TEMPL = 256
VBINS = 64
WAVE = 4096
OBLK = 128
ITERS = 1
ORBITS = 131072
SPAX = 128
TWAVE = 4160


def set_ends(result, rng, smallest, high):
    shape = result.shape
    place = [jax.random.randint(jax.random.fold_in(rng, axis), (), 0, shape[axis]) for axis in range(len(shape))]
    result = result.at[tuple(place)].set(smallest)
    longest = shape.index(max(shape))
    place[longest] = (place[longest] + 1) % shape[longest]
    return result.at[tuple(place)].set(high)


def shard_levels(rng, extent, shards, smallest, top_value):
    level, own = 1.0, jax.random.fold_in(rng, 6)
    for axis_at, blocks in shards:
        steps = jnp.exp(jax.random.uniform(jax.random.fold_in(own, axis_at), (blocks,), jnp.float32, smallest / len(shards), top_value / len(shards)))
        level = level * jnp.repeat(steps, extent[axis_at] // blocks).reshape([-1 if axis == axis_at else 1 for axis in range(len(extent))])
    return level


def scatter_about(rng, extent, scale, most, shards=(), kind=jnp.bfloat16):
    result = scale * jax.random.normal(rng, extent, jnp.float32)
    if shards:
        result = result * shard_levels(rng, extent, shards, -0.22, 0.18)
    return jnp.clip(result, -most, most).astype(kind)


def setup_inputs(seed: int = 0) -> dict:
    key_list = jax.random.split(jax.random.key(seed), 8)
    return {
        "weights": jnp.clip(jnp.exp(math.log(2.0) - 2.0794415 * jax.random.uniform(key_list[0], (ORBITS,), jnp.float32) ** shard_levels(key_list[0], (ORBITS,), ((0, 32),), -0.2, 0.2)), 0.25, 2.0),
        "losvd": jnp.clip(0.00390625 * jax.random.uniform(key_list[1], (ORBITS, SPAX, VBINS), jnp.float32) ** shard_levels(key_list[1], (ORBITS, SPAX, VBINS), ((0, 32), (1, 16)), -0.2, 0.2), 0.0, 0.00390625).astype(jnp.bfloat16),
        "occupancy": set_ends((jax.random.randint(key_list[2], (ORBITS // OBLK, SPAX), 0, 4) < 3).astype(jnp.int32), jax.random.fold_in(key_list[2], 1), 0, 1),
        "template_of": set_ends(jax.random.randint(key_list[3], (ORBITS,), 0, TEMPL), jax.random.fold_in(key_list[3], 1), 0, TEMPL - 1).astype(jnp.int32),
        "templates": scatter_about(key_list[4], (TEMPL, TWAVE), (TEMPL * VBINS) ** -0.5, 0.046875, ((0, 32),)),
        "observed": scatter_about(key_list[5], (SPAX, WAVE), 1.0, 6.0, ((0, 16),), jnp.float32),
        "inv_sigma": jnp.clip(jnp.exp(math.log(2.0) - 1.3862944 * jax.random.uniform(key_list[6], (SPAX, WAVE), jnp.float32) ** shard_levels(key_list[6], (SPAX, WAVE), ((0, 16),), -0.2, 0.2)), 0.5, 2.0),
    }


step_size = 0.5


def reference(weights, losvd, occupancy, template_of, templates, observed, inv_sigma):
    block_count = ORBITS // OBLK
    occupied = occupancy.astype(jnp.bfloat16)
    masked = (losvd.reshape(block_count, OBLK, SPAX, VBINS) * occupied[:, None, :, None]).reshape(block_count, OBLK, SPAX * VBINS)
    template_ids = template_of.reshape(block_count, OBLK)
    shift_list = jnp.arange(VBINS, dtype=jnp.int32)
    templates_wide = templates.astype(jnp.float32)

    def mixture_of(rounded):
        def accumulate(running, block_item):
            block_rows, block_ids, block_weights = block_item
            weighted = block_rows.astype(jnp.float32) * block_weights[:, None]
            return running + jax.ops.segment_sum(weighted, block_ids, num_segments=TEMPL), None

        start_sum = jnp.zeros((TEMPL, SPAX * VBINS), jnp.float32)
        summed, _ = lax.scan(accumulate, start_sum, (masked, template_ids, rounded.reshape(block_count, OBLK)))
        return summed.reshape(TEMPL, SPAX, VBINS)

    def model_of(mixture):
        def accumulate(running, shift_index):
            window = lax.dynamic_slice_in_dim(templates_wide, shift_index, WAVE, 1)
            column = lax.dynamic_index_in_dim(mixture, shift_index, 2, keepdims=False)
            return running + jnp.dot(column.T, window, preferred_element_type=jnp.float32, precision=lax.Precision.HIGHEST), None

        model, _ = lax.scan(accumulate, jnp.zeros((SPAX, WAVE), jnp.float32), shift_list)
        return model

    def response_of(scaled):
        def one_shift(unused, shift_index):
            window = lax.dynamic_slice_in_dim(templates, shift_index, WAVE, 1)
            return unused, jnp.dot(window, scaled.T, preferred_element_type=jnp.float32)

        _, stacked = lax.scan(one_shift, jnp.zeros((), jnp.float32), shift_list)
        return jnp.transpose(stacked, (1, 2, 0)).astype(jnp.bfloat16).reshape(TEMPL, SPAX * VBINS)

    def gradient_of(response):
        def one_block(unused, block_item):
            block_rows, block_ids = block_item
            picked = response[block_ids].astype(jnp.float32)
            return unused, jnp.sum(block_rows.astype(jnp.float32) * picked, axis=1)

        _, parts = lax.scan(one_block, jnp.zeros((), jnp.float32), (masked, template_ids))
        return parts.reshape(ORBITS)

    current = weights
    residual = jnp.zeros((SPAX, WAVE), jnp.float32)
    for iteration in range(ITERS):
        rounded = current.astype(jnp.bfloat16).astype(jnp.float32)
        mixture = mixture_of(rounded)
        model = model_of(mixture)
        residual = (model - observed) * inv_sigma
        scaled = (residual * inv_sigma).astype(jnp.bfloat16)
        response = response_of(scaled)
        gradient = gradient_of(response)
        current = jnp.maximum(current - step_size * gradient, 0.0)
    return current, residual
```

```python
import functools

import jax
import jax.numpy as jnp
from jax import lax
from jax.experimental import pallas as pl
from jax.experimental.pallas import tpu as pltpu
from jax.sharding import PartitionSpec as P

step_size = 0.5

GROUPS = 4
MEMBERS = 8
LANES = 128
VBINS = 64
WAVE = 4096
TWAVE = 4160
WIDE = 4224
TEMPL = 256
PAIR = 128
MIX_CHUNK = 1024
GRAD_CHUNK = 1024


def permuted(ids):
    return ((ids >> 3) & 7) * 32 + (ids >> 6) * 8 + (ids & 7)


def masked_rows(losvd_ref, occ_ref, chunk, step):
    blocks = chunk // LANES
    first = step * blocks
    block = lax.broadcasted_iota(jnp.int32, (occ_ref.shape[1], chunk), 0)
    orbit = lax.broadcasted_iota(jnp.int32, (occ_ref.shape[1], chunk), 1)
    spread = (block == first + orbit // LANES).astype(jnp.bfloat16)
    mask = jnp.dot(
        occ_ref[...].astype(jnp.bfloat16), spread, preferred_element_type=jnp.float32
    ).astype(jnp.bfloat16)
    rows = []
    for s in range(8):
        rows.append(losvd_ref[s] * jnp.broadcast_to(mask[s : s + 1, :], (VBINS, chunk)))
    return rows


def mix_kernel(losvd_ref, occ_ref, ids_ref, weights_ref, out_ref, acc_ref):
    step = pl.program_id(0)
    masked = jnp.concatenate(masked_rows(losvd_ref, occ_ref, MIX_CHUNK, step), axis=0)
    parts = []
    row = lax.broadcasted_iota(jnp.int32, (TEMPL, LANES), 0)
    for b in range(MIX_CHUNK // LANES):
        ids = permuted(ids_ref[b : b + 1, :])
        wide = weights_ref[b : b + 1, :].astype(jnp.bfloat16).astype(jnp.float32)
        parts.append(jnp.where(row == ids, wide, 0.0).astype(jnp.bfloat16))
    assign = jnp.concatenate(parts, axis=1)
    part = lax.dot_general(
        assign, masked, (((1,), (1,)), ((), ())), preferred_element_type=jnp.float32
    )

    @pl.when(step == 0)
    def _():
        acc_ref[...] = part

    @pl.when(step > 0)
    def _():
        acc_ref[...] += part

    @pl.when(step == pl.num_programs(0) - 1)
    def _():
        for k in range(GROUPS):
            for p in range(MEMBERS):
                out_ref[8 * k + p] = acc_ref[32 * p : 32 * p + 32, PAIR * k : PAIR * k + PAIR]


def mix(losvd, occ, ids, weights):
    steps = 4096 // MIX_CHUNK
    rows = MIX_CHUNK // LANES
    return pl.pallas_call(
        mix_kernel,
        name="mix",
        grid=(steps,),
        in_specs=[
            pl.BlockSpec((8, VBINS, MIX_CHUNK), lambda i: (0, 0, i)),
            pl.BlockSpec((8, 32), lambda i: (0, 0)),
            pl.BlockSpec((rows, LANES), lambda i: (i, 0)),
            pl.BlockSpec((rows, LANES), lambda i: (i, 0)),
        ],
        out_specs=pl.BlockSpec((32, 32, PAIR), lambda i: (0, 0, 0)),
        out_shape=jax.ShapeDtypeStruct((32, 32, PAIR), jnp.float32),
        scratch_shapes=[pltpu.VMEM((TEMPL, 8 * VBINS), jnp.float32)],
        compiler_params=pltpu.CompilerParams(vmem_limit_bytes=24 << 20),
        cost_estimate=pl.CostEstimate(flops=1 << 30, bytes_accessed=5 << 20, transcendentals=0),
    )(losvd, occ, ids, weights)


def three_terms(x):
    high = x.astype(jnp.bfloat16)
    rest = x - high.astype(jnp.float32)
    middle = rest.astype(jnp.bfloat16)
    low = (rest - middle.astype(jnp.float32)).astype(jnp.bfloat16)
    return jnp.concatenate([high, middle, low], axis=0)


def model_kernel(shares_ref, templates_ref, out_ref, wide_ref):
    mixture = shares_ref[0]
    for source in range(1, 32):
        mixture = mixture + shares_ref[source]
    terms = three_terms(mixture)
    templates = templates_ref[...].reshape(32, TWAVE)
    tripled = jnp.concatenate([templates, templates, templates], axis=0)
    over_templates = (((0,), (0,)), ((), ()))
    wide_ref[:, :WAVE] = lax.dot_general(
        terms, tripled[:, :WAVE], over_templates, preferred_element_type=jnp.float32
    )
    wide_ref[:, WAVE:TWAVE] = lax.dot_general(
        terms, tripled[:, WAVE:], over_templates, preferred_element_type=jnp.float32
    )
    for s in range(2):
        rows = wide_ref[VBINS * s : VBINS * s + VBINS, :]
        for half in (32, 16, 8):
            rows = rows[:half] + pltpu.roll(rows[half : 2 * half], WIDE - half, 1)
        for half in (4, 2, 1):
            rows = rows + pltpu.roll(pltpu.roll(rows, 8 - half, 0), WIDE - half, 1)
        for q in range(4):
            piece = rows[0:1, 1024 * q : 1024 * q + 1024]
            for member in range(MEMBERS):
                out_ref[member, 4 * s + q : 4 * s + q + 1, :] = piece


def model(shares, templates):
    return pl.pallas_call(
        model_kernel,
        name="model",
        out_shape=jax.ShapeDtypeStruct((MEMBERS, 8, 1024), jnp.float32),
        scratch_shapes=[pltpu.VMEM((PAIR, WIDE), jnp.float32)],
        compiler_params=pltpu.CompilerParams(vmem_limit_bytes=24 << 20),
        cost_estimate=pl.CostEstimate(flops=1 << 27, bytes_accessed=1 << 20, transcendentals=0),
    )(shares, templates)


def respond_kernel(place_ref, parts_ref, observed_ref, sigma_ref, templates_ref, out_ref, res_ref, shift_ref):
    k = place_ref[0]
    p = place_ref[1]
    total = parts_ref[0]
    for member in range(1, MEMBERS):
        total = total + parts_ref[member]
    templates = templates_ref[...].reshape(32, TWAVE)
    for s in range(2):
        spectrum = jnp.concatenate([total[4 * s + q : 4 * s + q + 1, :] for q in range(4)], axis=1)
        inverse = sigma_ref[pl.ds(2 * k + s, 1), :]
        residual = (spectrum - observed_ref[pl.ds(2 * k + s, 1), :]) * inverse
        res_ref[s : s + 1, :] = residual
        scaled = (residual * inverse).astype(jnp.bfloat16).astype(jnp.float32)
        padded = jnp.concatenate([scaled, jnp.zeros((1, WIDE - WAVE), jnp.float32)], axis=1)
        spread = jnp.broadcast_to(padded, (VBINS, WIDE))
        shift_ref[VBINS * s : VBINS * s + VBINS, :] = pltpu.roll(
            spread, 0, 1, stride=1, stride_axis=0
        ).astype(jnp.bfloat16)
    over_waves = (((1,), (1,)), ((), ()))
    response = lax.dot_general(
        templates[:, :WAVE], shift_ref[:, :WAVE], over_waves, preferred_element_type=jnp.float32
    )
    response = response + lax.dot_general(
        templates[:, WAVE:], shift_ref[:, WAVE:TWAVE], over_waves, preferred_element_type=jnp.float32
    )
    share = res_ref[:, pl.ds(pl.multiple_of(p * 512, 512), 512)]
    share = jnp.concatenate([share[:, LANES * j : LANES * j + LANES] for j in range(4)], axis=0)
    high = share.astype(jnp.bfloat16)
    low = (share - high.astype(jnp.float32)).astype(jnp.bfloat16)
    message = jnp.concatenate([response.astype(jnp.bfloat16), high, low], axis=0)
    for target in range(32):
        out_ref[target] = message


def respond(place, parts, observed, sigma, templates):
    vmem = pl.BlockSpec(memory_space=pltpu.VMEM)
    return pl.pallas_call(
        respond_kernel,
        name="respond",
        in_specs=[pl.BlockSpec(memory_space=pltpu.SMEM), vmem, vmem, vmem, vmem],
        out_shape=jax.ShapeDtypeStruct((32, 48, PAIR), jnp.bfloat16),
        scratch_shapes=[
            pltpu.VMEM((2, WAVE), jnp.float32),
            pltpu.VMEM((PAIR, WIDE), jnp.bfloat16),
        ],
        compiler_params=pltpu.CompilerParams(vmem_limit_bytes=24 << 20),
        cost_estimate=pl.CostEstimate(flops=1 << 27, bytes_accessed=1 << 20, transcendentals=0),
    )(place, parts, observed, sigma, templates)


def grad_kernel(losvd_ref, occ_ref, ids_ref, message_ref, out_ref, res_ref, table_ref):
    step = pl.program_id(0)

    @pl.when(step == 0)
    def _():
        for k in range(GROUPS):
            table_ref[:, PAIR * k : PAIR * k + PAIR] = message_ref[8 * k : 8 * k + 8, 0:32, :].reshape(
                TEMPL, PAIR
            )
            for p in range(MEMBERS):
                terms = message_ref[8 * k + p, 32:48, :].astype(jnp.float32)
                share = terms[0:8] + terms[8:16]
                for j in range(4):
                    at = LANES * (4 * p + j)
                    res_ref[2 * k : 2 * k + 2, at : at + LANES] = share[2 * j : 2 * j + 2]

    masked = jnp.concatenate(masked_rows(losvd_ref, occ_ref, GRAD_CHUNK, step), axis=0)
    scores = jnp.dot(table_ref[...], masked, preferred_element_type=jnp.float32)
    row = lax.broadcasted_iota(jnp.int32, (TEMPL, LANES), 0)
    sums = []
    for b in range(GRAD_CHUNK // LANES):
        ids = permuted(ids_ref[b : b + 1, :])
        picked = jnp.where(row == ids, scores[:, LANES * b : LANES * b + LANES], 0.0)
        sums.append(jnp.sum(picked, axis=0, keepdims=True))
    gradient = jnp.concatenate(sums, axis=0)
    for target in range(16):
        out_ref[target] = gradient


def grad(losvd, occ, ids, message):
    steps = 4096 // GRAD_CHUNK
    rows = GRAD_CHUNK // LANES
    return pl.pallas_call(
        grad_kernel,
        name="grad",
        grid=(steps,),
        in_specs=[
            pl.BlockSpec((8, VBINS, GRAD_CHUNK), lambda i: (0, 0, i)),
            pl.BlockSpec((8, 32), lambda i: (0, 0)),
            pl.BlockSpec((rows, LANES), lambda i: (i, 0)),
            pl.BlockSpec((32, 48, PAIR), lambda i: (0, 0, 0)),
        ],
        out_specs=[
            pl.BlockSpec((16, rows, LANES), lambda i: (0, i, 0)),
            pl.BlockSpec((8, WAVE), lambda i: (0, 0)),
        ],
        out_shape=[
            jax.ShapeDtypeStruct((16, 32, LANES), jnp.float32),
            jax.ShapeDtypeStruct((8, WAVE), jnp.float32),
        ],
        scratch_shapes=[pltpu.VMEM((TEMPL, 8 * VBINS), jnp.bfloat16)],
        compiler_params=pltpu.CompilerParams(vmem_limit_bytes=24 << 20),
        cost_estimate=pl.CostEstimate(flops=1 << 30, bytes_accessed=5 << 20, transcendentals=0),
    )(losvd, occ, ids, message)


def update_kernel(weights_ref, parts_ref, out_ref):
    total = parts_ref[0]
    for source in range(1, 16):
        total = total + parts_ref[source]
    out_ref[...] = jnp.maximum(weights_ref[...] - step_size * total, 0.0)


def update(weights, parts):
    return pl.pallas_call(
        update_kernel,
        name="update",
        out_shape=jax.ShapeDtypeStruct((32, LANES), jnp.float32),
        compiler_params=pltpu.CompilerParams(vmem_limit_bytes=8 << 20),
    )(weights, parts)


def local(weights, losvd, occupancy, template_of, templates, observed, inv_sigma):
    exchange = functools.partial(lax.all_to_all, split_axis=0, concat_axis=0, tiled=True)
    same_member = [[MEMBERS * k + p for k in range(GROUPS)] for p in range(MEMBERS)]
    same_group = [[MEMBERS * k + p for p in range(MEMBERS)] for k in range(GROUPS)]
    rows = losvd.transpose(1, 2, 0)
    occ = occupancy.T
    ids = template_of.reshape(32, LANES)
    now = weights.reshape(32, LANES)
    index = lax.axis_index("orb")
    place = jnp.stack([index // MEMBERS, index % MEMBERS]).astype(jnp.int32)
    own = jnp.broadcast_to(templates, (GROUPS, *templates.shape))
    gathered = exchange(own, "orb", axis_index_groups=same_member)
    shares = exchange(mix(rows, occ, ids, now), "orb")
    parts = exchange(model(shares, gathered), "orb", axis_index_groups=same_group)
    message = exchange(respond(place, parts, observed, inv_sigma, gathered), "orb")
    gradient, residual = grad(rows, occ, ids, message)
    sums = exchange(gradient, "spx")
    return update(now, sums).reshape(weights.shape), residual


def solution(mesh):
    placed = (
        P("orb"),
        P("orb", "spx", None),
        P("orb", "spx"),
        P("orb"),
        P("orb", None),
        P("spx", None),
        P("spx", None),
    )
    return jax.shard_map(
        local, mesh=mesh, in_specs=placed, out_specs=(P("orb"), P("spx", None)), check_vma=False
    )
```

```python
import functools

import jax
import jax.numpy as jnp
from jax import lax
from jax.experimental import pallas as pl
from jax.experimental.pallas import tpu as pltpu
from jax.sharding import PartitionSpec as P

step_size = 0.5

GROUPS = 4
MEMBERS = 8
LANES = 128
VBINS = 64
WAVE = 4096
TWAVE = 4160
WIDE = 4224
TEMPL = 256
PAIR = 128
MIX_CHUNK = 512
HELD = 2048
GRAD_CHUNK = 1024
MIX_SCALE = 8192.0
GRAD_SCALE = 16.0


def masked_rows(rows, mask):
    parts = [rows[s] * jnp.broadcast_to(mask[s : s + 1, :], rows.shape[1:]) for s in range(8)]
    return jnp.concatenate(parts, axis=0)


def mask_of(occ, first, count):
    block = lax.broadcasted_iota(jnp.int32, (occ.shape[1], count), 0)
    orbit = lax.broadcasted_iota(jnp.int32, (occ.shape[1], count), 1)
    spread = (block == (first + orbit) // LANES).astype(jnp.bfloat16)
    return jnp.dot(
        occ.astype(jnp.bfloat16), spread, preferred_element_type=jnp.float32
    ).astype(jnp.bfloat16)


def mix_kernel(
    losvd_ref, occ_ref, ids_ref, weights_ref, out_ref, masked_ref, rows_ref, occ_buf, ids_buf, weights_buf, acc_ref, sems
):
    copies = [
        pltpu.make_async_copy(occ_ref, occ_buf, sems.at[0]),
        pltpu.make_async_copy(ids_ref, ids_buf, sems.at[1]),
        pltpu.make_async_copy(weights_ref, weights_buf, sems.at[2]),
    ]
    chunks = 4096 // MIX_CHUNK
    for c in range(chunks):
        source = losvd_ref.at[:, :, pl.ds(MIX_CHUNK * c, MIX_CHUNK)]
        copies.append(pltpu.make_async_copy(source, rows_ref.at[c], sems.at[3 + c]))
    for copy in copies:
        copy.start()
    for copy in copies[:3]:
        copy.wait()
    row = lax.broadcasted_iota(jnp.int32, (TEMPL, LANES), 0)
    blocks = MIX_CHUNK // LANES
    for c in range(chunks):
        parts = []
        for b in range(blocks * c, blocks * (c + 1)):
            ids = ids_buf[b : b + 1, :]
            wide = weights_buf[b : b + 1, :].astype(jnp.bfloat16).astype(jnp.float32)
            parts.append(jnp.where(row == ids, wide, 0.0).astype(jnp.bfloat16))
        assign = jnp.concatenate(parts, axis=1)
        mask = mask_of(occ_buf[...], MIX_CHUNK * c, MIX_CHUNK)
        copies[3 + c].wait()
        masked = masked_rows(rows_ref[c], mask)
        if MIX_CHUNK * c < HELD:
            masked_ref[:, MIX_CHUNK * c : MIX_CHUNK * (c + 1)] = masked
        part = lax.dot_general(
            assign, masked, (((1,), (1,)), ((), ())), preferred_element_type=jnp.float32
        )
        if c == 0:
            acc_ref[...] = part
        elif c < chunks - 1:
            acc_ref[...] += part
        else:
            acc_ref[...] = jnp.sqrt(acc_ref[...] + part) * MIX_SCALE
    for k in range(GROUPS):
        for p in range(MEMBERS):
            out_ref[GROUPS * p + k] = acc_ref[32 * p : 32 * p + 32, PAIR * k : PAIR * k + PAIR]


def mix(losvd, occ, ids, weights):
    hbm = pl.BlockSpec(memory_space=pltpu.HBM)
    vmem = pl.BlockSpec(memory_space=pltpu.VMEM)
    chunks = 4096 // MIX_CHUNK
    return pl.pallas_call(
        mix_kernel,
        name="mix",
        in_specs=[hbm] * 4,
        out_specs=[vmem, vmem],
        out_shape=[
            jax.ShapeDtypeStruct((32, 32, PAIR), jnp.float32),
            jax.ShapeDtypeStruct((8 * VBINS, HELD), jnp.bfloat16),
        ],
        scratch_shapes=[
            pltpu.VMEM((chunks, 8, VBINS, MIX_CHUNK), jnp.bfloat16),
            pltpu.VMEM((8, 32), jnp.int32),
            pltpu.VMEM((32, LANES), jnp.int32),
            pltpu.VMEM((32, LANES), jnp.float32),
            pltpu.VMEM((TEMPL, 8 * VBINS), jnp.float32),
            pltpu.SemaphoreType.DMA((3 + chunks,)),
        ],
        compiler_params=pltpu.CompilerParams(vmem_limit_bytes=16 << 20),
        cost_estimate=pl.CostEstimate(flops=1 << 30, bytes_accessed=5 << 20, transcendentals=0),
    )(*(pltpu.with_memory_space_constraint(x, pltpu.HBM) for x in (losvd, occ, ids, weights)))


def three_terms(x):
    high = x.astype(jnp.bfloat16)
    rest = x - high.astype(jnp.float32)
    middle = rest.astype(jnp.bfloat16)
    low = (rest - middle.astype(jnp.float32)).astype(jnp.bfloat16)
    return jnp.concatenate([high, middle, low], axis=0)


def whereabouts():
    index = lax.axis_index("orb")
    return lax.rem(index, GROUPS)


def own_order(k):
    return [pl.multiple_of(8 * jnp.bitwise_xor(k, j), 8) for j in range(GROUPS)]


def model_kernel(mixture_ref, t0_ref, t1_ref, t2_ref, t3_ref, out_ref, all_ref, wide_ref):
    mixture = jnp.concatenate([mixture_ref[pl.ds(at, 8), :] for at in own_order(whereabouts())], axis=0)
    terms = three_terms(mixture)
    templates = jnp.concatenate([t0_ref[...], t1_ref[...], t2_ref[...], t3_ref[...]], axis=0)
    all_ref[...] = templates
    tripled = jnp.concatenate([templates, templates, templates], axis=0)
    over_templates = (((0,), (0,)), ((), ()))
    wide_ref[:, :WAVE] = lax.dot_general(
        terms, tripled[:, :WAVE], over_templates, preferred_element_type=jnp.float32
    )
    wide_ref[:, WAVE:TWAVE] = lax.dot_general(
        terms, tripled[:, WAVE:], over_templates, preferred_element_type=jnp.float32
    )
    for s in range(2):
        rows = wide_ref[VBINS * s : VBINS * s + VBINS, :]
        for half in (32, 16, 8):
            rows = rows[:half] + pltpu.roll(rows[half : 2 * half], WIDE - half, 1)
        for half in (4, 2, 1):
            rows = rows + pltpu.roll(pltpu.roll(rows, 8 - half, 0), WIDE - half, 1)
        for q in range(4):
            piece = rows[0:1, 1024 * q : 1024 * q + 1024]
            for member in range(MEMBERS):
                out_ref[member, 4 * s + q : 4 * s + q + 1, :] = piece


def model(mixture, templates):
    vmem = pl.BlockSpec(memory_space=pltpu.VMEM)
    return pl.pallas_call(
        model_kernel,
        name="model",
        in_specs=[vmem] * 5,
        out_shape=[
            jax.ShapeDtypeStruct((MEMBERS, 8, 1024), jnp.float32),
            jax.ShapeDtypeStruct((32, TWAVE), jnp.bfloat16),
        ],
        scratch_shapes=[pltpu.VMEM((PAIR, WIDE), jnp.float32)],
        compiler_params=pltpu.CompilerParams(vmem_limit_bytes=24 << 20),
        cost_estimate=pl.CostEstimate(flops=1 << 27, bytes_accessed=1 << 20, transcendentals=0),
    )(mixture, *templates)


def respond_kernel(parts_ref, observed_ref, sigma_ref, templates_ref, out_ref, res_ref, shift_ref, rows_ref):
    k = whereabouts()
    total = parts_ref[0]
    for member in range(1, MEMBERS):
        total = total + parts_ref[member]
    templates = templates_ref[...]
    for s in range(2):
        spectrum = jnp.concatenate([total[4 * s + q : 4 * s + q + 1, :] for q in range(4)], axis=1)
        inverse = sigma_ref[pl.ds(2 * k + s, 1), :]
        residual = (spectrum - observed_ref[pl.ds(2 * k + s, 1), :]) * inverse
        for q in range(4):
            res_ref[4 * s + q : 4 * s + q + 1, :] = residual[:, 1024 * q : 1024 * q + 1024]
        scaled = (residual * inverse).astype(jnp.bfloat16).astype(jnp.float32)
        padded = jnp.concatenate([scaled, jnp.zeros((1, WIDE - WAVE), jnp.float32)], axis=1)
        spread = jnp.broadcast_to(padded, (VBINS, WIDE))
        shift_ref[VBINS * s : VBINS * s + VBINS, :] = pltpu.roll(
            spread, 0, 1, stride=1, stride_axis=0
        ).astype(jnp.bfloat16)
    over_waves = (((1,), (1,)), ((), ()))
    response = lax.dot_general(
        templates[:, :WAVE], shift_ref[:, :WAVE], over_waves, preferred_element_type=jnp.float32
    )
    response = response + lax.dot_general(
        templates[:, WAVE:], shift_ref[:, WAVE:TWAVE], over_waves, preferred_element_type=jnp.float32
    )
    for j, at in enumerate(own_order(k)):
        rows_ref[pl.ds(at, 8), :] = response[8 * j : 8 * j + 8]
    message = rows_ref[...].astype(jnp.bfloat16)
    for target in range(32):
        out_ref[target] = message


def respond(parts, observed, sigma, templates):
    vmem = pl.BlockSpec(memory_space=pltpu.VMEM)
    return pl.pallas_call(
        respond_kernel,
        name="respond",
        in_specs=[vmem] * 4,
        out_shape=[
            jax.ShapeDtypeStruct((32, 32, PAIR), jnp.bfloat16),
            jax.ShapeDtypeStruct((8, 1024), jnp.float32),
        ],
        scratch_shapes=[
            pltpu.VMEM((PAIR, WIDE), jnp.bfloat16),
            pltpu.VMEM((32, PAIR), jnp.float32),
        ],
        compiler_params=pltpu.CompilerParams(vmem_limit_bytes=24 << 20),
        cost_estimate=pl.CostEstimate(flops=1 << 27, bytes_accessed=1 << 20, transcendentals=0),
    )(parts, observed, sigma, templates)


def grad_kernel(
    masked_ref, losvd_ref, occ_ref, ids_ref, message_ref, after_ref, out_ref, table_ref, rows_ref, sems
):
    chunks = 4096 // GRAD_CHUNK
    held = HELD // GRAD_CHUNK
    copies = []
    for c in range(held, chunks):
        source = losvd_ref.at[:, :, pl.ds(GRAD_CHUNK * c, GRAD_CHUNK)]
        copies.append(pltpu.make_async_copy(source, rows_ref.at[c - held], sems.at[c - held]))
    for copy in copies:
        copy.start()
    for k in range(GROUPS):
        for p in range(MEMBERS):
            table_ref[32 * p : 32 * p + 32, PAIR * k : PAIR * k + PAIR] = message_ref[GROUPS * p + k]
    row = lax.broadcasted_iota(jnp.int32, (TEMPL, LANES), 0)
    for c in range(chunks):
        if c < held:
            masked = masked_ref[:, GRAD_CHUNK * c : GRAD_CHUNK * (c + 1)]
        else:
            mask = mask_of(occ_ref[...], GRAD_CHUNK * c, GRAD_CHUNK)
            copies[c - held].wait()
            masked = masked_rows(rows_ref[c - held], mask)
        scores = jnp.dot(table_ref[...], masked, preferred_element_type=jnp.float32)
        for b in range(GRAD_CHUNK // LANES):
            at = GRAD_CHUNK // LANES * c + b
            ids = ids_ref[at : at + 1, :]
            picked = jnp.where(row == ids, scores[:, LANES * b : LANES * b + LANES], 0.0)
            gradient = jnp.sum(picked, axis=0, keepdims=True)
            root = jnp.sqrt(jnp.abs(gradient)) * GRAD_SCALE
            out_ref[at : at + 1, :] = jnp.where(gradient < 0.0, -root, root)


def grad(masked, losvd, occ, ids, message, after):
    hbm = pl.BlockSpec(memory_space=pltpu.HBM)
    vmem = pl.BlockSpec(memory_space=pltpu.VMEM)
    fetched = max((4096 - HELD) // GRAD_CHUNK, 1)
    return pl.pallas_call(
        grad_kernel,
        name="grad",
        in_specs=[vmem, hbm, vmem, vmem, vmem, hbm],
        out_specs=vmem,
        out_shape=jax.ShapeDtypeStruct((32, LANES), jnp.float32),
        scratch_shapes=[
            pltpu.VMEM((TEMPL, 8 * VBINS), jnp.bfloat16),
            pltpu.VMEM((fetched, 8, VBINS, GRAD_CHUNK), jnp.bfloat16),
            pltpu.SemaphoreType.DMA((fetched,)),
        ],
        compiler_params=pltpu.CompilerParams(vmem_limit_bytes=16 << 20),
        cost_estimate=pl.CostEstimate(flops=1 << 30, bytes_accessed=5 << 20, transcendentals=0),
    )(masked, pltpu.with_memory_space_constraint(losvd, pltpu.HBM), occ, ids, message, after)


def assemble_kernel(r0_ref, r1_ref, r2_ref, r3_ref, out_ref):
    k = whereabouts()
    pieces = [r0_ref[...], r1_ref[...], r2_ref[...], r3_ref[...]]
    for group in range(GROUPS):
        j = jnp.bitwise_xor(k, group)
        piece = jnp.where(
            j < 2, jnp.where(j == 0, pieces[0], pieces[1]), jnp.where(j == 2, pieces[2], pieces[3])
        )
        for s in range(2):
            for q in range(4):
                out_ref[2 * group + s : 2 * group + s + 1, 1024 * q : 1024 * q + 1024] = piece[
                    4 * s + q : 4 * s + q + 1, :
                ]


def assemble(pieces):
    vmem = pl.BlockSpec(memory_space=pltpu.VMEM)
    return pl.pallas_call(
        assemble_kernel,
        name="assemble",
        in_specs=[vmem] * 4,
        out_shape=jax.ShapeDtypeStruct((8, WAVE), jnp.float32),
        compiler_params=pltpu.CompilerParams(vmem_limit_bytes=4 << 20),
    )(*pieces)


def step(weights, losvd, occupancy, template_of, templates, observed, inv_sigma):
    exchange = functools.partial(lax.all_to_all, split_axis=0, concat_axis=0, tiled=True)
    same_spaxels = [[GROUPS * p + k for p in range(MEMBERS)] for k in range(GROUPS)]
    rows = losvd.transpose(1, 2, 0)
    occ = occupancy.T
    ids = template_of.reshape(32, LANES)
    now = weights.reshape(32, LANES)

    def from_group(array, j):
        return lax.ppermute(array, "orb", [(i, i ^ j) for i in range(32)])

    gathered = [templates] + [from_group(templates, j) for j in range(1, GROUPS)]
    mixed, masked = mix(rows, occ, ids, now)
    shares = exchange(mixed.astype(jnp.float16), "orb").astype(jnp.float32)
    mixture = jnp.sum(shares * shares, axis=0) * (1.0 / MIX_SCALE**2)
    spectra, wanted = model(mixture, gathered)
    parts = exchange(spectra, "orb", axis_index_groups=same_spaxels)
    response, part = respond(parts, observed, inv_sigma, wanted)
    message = exchange(response, "orb")
    residual = assemble([part] + [from_group(part, j) for j in range(1, GROUPS)])
    roots = grad(masked, rows, occ, ids, message, residual).astype(jnp.float16)
    sums = exchange(jnp.broadcast_to(roots, (16, 32, LANES)), "spx").astype(jnp.float32)
    moved = jnp.sum(sums * jnp.abs(sums), axis=0) * (1.0 / GRAD_SCALE**2)
    return jnp.maximum(now - step_size * moved, 0.0).reshape(weights.shape), residual


def solution(mesh):
    placed = (
        P("orb"),
        P("orb", "spx", None),
        P("orb", "spx"),
        P("orb"),
        P("orb", None),
        P("spx", None),
        P("spx", None),
    )
    return jax.shard_map(
        step, mesh=mesh, in_specs=placed, out_specs=(P("orb"), P("spx", None)), check_vma=False
    )
```

```python
import functools

import jax
import jax.numpy as jnp
from jax import lax
from jax.experimental import pallas as pl
from jax.experimental.pallas import tpu as pltpu
from jax.sharding import PartitionSpec as P

step_size = 0.5

GROUPS = 4
MEMBERS = 8
LANES = 128
VBINS = 64
WAVE = 4096
TWAVE = 4160
WIDE = 4224
TEMPL = 256
PAIR = 128
MIX_CHUNK = 1024
HELD = 2048
GRAD_CHUNK = 1024
MIX_SCALE = 8192.0
GRAD_SCALE = 16.0
SPECTRUM_SCALE = 16.0


def masked_rows(rows, mask):
    parts = [rows[s] * jnp.broadcast_to(mask[s : s + 1, :], rows.shape[1:]) for s in range(8)]
    return jnp.concatenate(parts, axis=0)


def mask_of(occ, first, count):
    block = lax.broadcasted_iota(jnp.int32, (occ.shape[1], count), 0)
    orbit = lax.broadcasted_iota(jnp.int32, (occ.shape[1], count), 1)
    spread = (block == (first + orbit) // LANES).astype(jnp.bfloat16)
    return jnp.dot(
        occ.astype(jnp.bfloat16), spread, preferred_element_type=jnp.float32
    ).astype(jnp.bfloat16)


def mix_kernel(
    losvd_ref, occ_ref, ids_ref, weights_ref, out_ref, masked_ref, rows_ref, occ_buf, ids_buf, weights_buf, acc_ref, sems
):
    copies = [
        pltpu.make_async_copy(occ_ref, occ_buf, sems.at[0]),
        pltpu.make_async_copy(ids_ref, ids_buf, sems.at[1]),
        pltpu.make_async_copy(weights_ref, weights_buf, sems.at[2]),
    ]
    chunks = 4096 // MIX_CHUNK
    for c in range(chunks):
        source = losvd_ref.at[:, :, pl.ds(MIX_CHUNK * c, MIX_CHUNK)]
        copies.append(pltpu.make_async_copy(source, rows_ref.at[c], sems.at[3 + c]))
    for copy in copies:
        copy.start()
    for copy in copies[:3]:
        copy.wait()
    row = lax.broadcasted_iota(jnp.int32, (TEMPL, LANES), 0)
    blocks = MIX_CHUNK // LANES
    for c in range(chunks):
        parts = []
        for b in range(blocks * c, blocks * (c + 1)):
            ids = ids_buf[b : b + 1, :]
            wide = weights_buf[b : b + 1, :].astype(jnp.bfloat16).astype(jnp.float32)
            parts.append(jnp.where(row == ids, wide, 0.0).astype(jnp.bfloat16))
        assign = jnp.concatenate(parts, axis=1)
        mask = mask_of(occ_buf[...], MIX_CHUNK * c, MIX_CHUNK)
        copies[3 + c].wait()
        masked = masked_rows(rows_ref[c], mask)
        if MIX_CHUNK * c < HELD:
            masked_ref[:, MIX_CHUNK * c : MIX_CHUNK * (c + 1)] = masked
        part = lax.dot_general(
            assign, masked, (((1,), (1,)), ((), ())), preferred_element_type=jnp.float32
        )
        if c == 0:
            acc_ref[...] = part
        elif c < chunks - 1:
            acc_ref[...] += part
        else:
            acc_ref[...] = jnp.sqrt(acc_ref[...] + part) * MIX_SCALE
    for k in range(GROUPS):
        for p in range(MEMBERS):
            out_ref[GROUPS * p + k] = acc_ref[32 * p : 32 * p + 32, PAIR * k : PAIR * k + PAIR]


def mix(losvd, occ, ids, weights):
    hbm = pl.BlockSpec(memory_space=pltpu.HBM)
    vmem = pl.BlockSpec(memory_space=pltpu.VMEM)
    chunks = 4096 // MIX_CHUNK
    return pl.pallas_call(
        mix_kernel,
        name="mix",
        in_specs=[hbm] * 4,
        out_specs=[vmem, vmem],
        out_shape=[
            jax.ShapeDtypeStruct((32, 32, PAIR), jnp.float32),
            jax.ShapeDtypeStruct((8 * VBINS, HELD), jnp.bfloat16),
        ],
        scratch_shapes=[
            pltpu.VMEM((chunks, 8, VBINS, MIX_CHUNK), jnp.bfloat16),
            pltpu.VMEM((8, 32), jnp.int32),
            pltpu.VMEM((32, LANES), jnp.int32),
            pltpu.VMEM((32, LANES), jnp.float32),
            pltpu.VMEM((TEMPL, 8 * VBINS), jnp.float32),
            pltpu.SemaphoreType.DMA((3 + chunks,)),
        ],
        compiler_params=pltpu.CompilerParams(vmem_limit_bytes=16 << 20),
        cost_estimate=pl.CostEstimate(flops=1 << 30, bytes_accessed=5 << 20, transcendentals=0),
    )(*(pltpu.with_memory_space_constraint(x, pltpu.HBM) for x in (losvd, occ, ids, weights)))


def three_terms(x):
    high = x.astype(jnp.bfloat16)
    rest = x - high.astype(jnp.float32)
    middle = rest.astype(jnp.bfloat16)
    low = (rest - middle.astype(jnp.float32)).astype(jnp.bfloat16)
    return jnp.concatenate([high, middle, low], axis=0)


def whereabouts():
    index = lax.axis_index("orb")
    return lax.rem(index, GROUPS)


def own_order(k):
    return [pl.multiple_of(8 * jnp.bitwise_xor(k, j), 8) for j in range(GROUPS)]


def model_kernel(mixture_ref, t0_ref, t1_ref, t2_ref, t3_ref, out_ref, all_ref, wide_ref):
    mixture = jnp.concatenate([mixture_ref[pl.ds(at, 8), :] for at in own_order(whereabouts())], axis=0)
    terms = three_terms(mixture)
    templates = jnp.concatenate([t0_ref[...], t1_ref[...], t2_ref[...], t3_ref[...]], axis=0)
    all_ref[...] = templates
    tripled = jnp.concatenate([templates, templates, templates], axis=0)
    over_templates = (((0,), (0,)), ((), ()))
    wide_ref[:, :WAVE] = lax.dot_general(
        terms, tripled[:, :WAVE], over_templates, preferred_element_type=jnp.float32
    )
    wide_ref[:, WAVE:TWAVE] = lax.dot_general(
        terms, tripled[:, WAVE:], over_templates, preferred_element_type=jnp.float32
    )
    for s in range(2):
        rows = wide_ref[VBINS * s : VBINS * s + VBINS, :]
        for half in (32, 16, 8):
            rows = rows[:half] + pltpu.roll(rows[half : 2 * half], WIDE - half, 1)
        for half in (4, 2, 1):
            rows = rows + pltpu.roll(pltpu.roll(rows, 8 - half, 0), WIDE - half, 1)
        for q in range(4):
            piece = rows[0:1, 1024 * q : 1024 * q + 1024]
            for member in range(MEMBERS):
                out_ref[member, 4 * s + q : 4 * s + q + 1, :] = piece


def model(mixture, templates):
    vmem = pl.BlockSpec(memory_space=pltpu.VMEM)
    return pl.pallas_call(
        model_kernel,
        name="model",
        in_specs=[vmem] * 5,
        out_shape=[
            jax.ShapeDtypeStruct((MEMBERS, 8, 1024), jnp.float32),
            jax.ShapeDtypeStruct((32, TWAVE), jnp.bfloat16),
        ],
        scratch_shapes=[pltpu.VMEM((PAIR, WIDE), jnp.float32)],
        compiler_params=pltpu.CompilerParams(vmem_limit_bytes=24 << 20),
        cost_estimate=pl.CostEstimate(flops=1 << 27, bytes_accessed=1 << 20, transcendentals=0),
    )(mixture, *templates)


def respond_kernel(parts_ref, observed_ref, sigma_ref, templates_ref, out_ref, res_ref, shift_ref, rows_ref):
    k = whereabouts()
    total = parts_ref[...]
    templates = templates_ref[...]
    for s in range(2):
        spectrum = jnp.concatenate([total[4 * s + q : 4 * s + q + 1, :] for q in range(4)], axis=1)
        inverse = sigma_ref[pl.ds(2 * k + s, 1), :]
        residual = (spectrum - observed_ref[pl.ds(2 * k + s, 1), :]) * inverse
        for q in range(4):
            res_ref[4 * s + q : 4 * s + q + 1, :] = residual[:, 1024 * q : 1024 * q + 1024]
        scaled = (residual * inverse).astype(jnp.bfloat16).astype(jnp.float32)
        padded = jnp.concatenate([scaled, jnp.zeros((1, WIDE - WAVE), jnp.float32)], axis=1)
        spread = jnp.broadcast_to(padded, (VBINS, WIDE))
        shift_ref[VBINS * s : VBINS * s + VBINS, :] = pltpu.roll(
            spread, 0, 1, stride=1, stride_axis=0
        ).astype(jnp.bfloat16)
    over_waves = (((1,), (1,)), ((), ()))
    response = lax.dot_general(
        templates[:, :WAVE], shift_ref[:, :WAVE], over_waves, preferred_element_type=jnp.float32
    )
    response = response + lax.dot_general(
        templates[:, WAVE:], shift_ref[:, WAVE:TWAVE], over_waves, preferred_element_type=jnp.float32
    )
    for j, at in enumerate(own_order(k)):
        rows_ref[pl.ds(at, 8), :] = response[8 * j : 8 * j + 8]
    message = rows_ref[...].astype(jnp.bfloat16)
    for target in range(32):
        out_ref[target] = message


def respond(parts, observed, sigma, templates):
    vmem = pl.BlockSpec(memory_space=pltpu.VMEM)
    return pl.pallas_call(
        respond_kernel,
        name="respond",
        in_specs=[vmem] * 4,
        out_shape=[
            jax.ShapeDtypeStruct((32, 32, PAIR), jnp.bfloat16),
            jax.ShapeDtypeStruct((8, 1024), jnp.float32),
        ],
        scratch_shapes=[
            pltpu.VMEM((PAIR, WIDE), jnp.bfloat16),
            pltpu.VMEM((32, PAIR), jnp.float32),
        ],
        compiler_params=pltpu.CompilerParams(vmem_limit_bytes=24 << 20),
        cost_estimate=pl.CostEstimate(flops=1 << 27, bytes_accessed=1 << 20, transcendentals=0),
    )(parts, observed, sigma, templates)


def grad_kernel(
    masked_ref, losvd_ref, occ_ref, ids_ref, message_ref, after_ref, out_ref, table_ref, rows_ref, sems
):
    chunks = 4096 // GRAD_CHUNK
    held = HELD // GRAD_CHUNK
    copies = []
    for c in range(held, chunks):
        source = losvd_ref.at[:, :, pl.ds(GRAD_CHUNK * c, GRAD_CHUNK)]
        copies.append(pltpu.make_async_copy(source, rows_ref.at[c - held], sems.at[c - held]))
    for copy in copies:
        copy.start()
    for k in range(GROUPS):
        for p in range(MEMBERS):
            table_ref[32 * p : 32 * p + 32, PAIR * k : PAIR * k + PAIR] = message_ref[GROUPS * p + k]
    row = lax.broadcasted_iota(jnp.int32, (TEMPL, LANES), 0)
    for c in range(chunks):
        if c < held:
            masked = masked_ref[:, GRAD_CHUNK * c : GRAD_CHUNK * (c + 1)]
        else:
            mask = mask_of(occ_ref[...], GRAD_CHUNK * c, GRAD_CHUNK)
            copies[c - held].wait()
            masked = masked_rows(rows_ref[c - held], mask)
        scores = jnp.dot(table_ref[...], masked, preferred_element_type=jnp.float32)
        for b in range(GRAD_CHUNK // LANES):
            at = GRAD_CHUNK // LANES * c + b
            ids = ids_ref[at : at + 1, :]
            picked = jnp.where(row == ids, scores[:, LANES * b : LANES * b + LANES], 0.0)
            gradient = jnp.sum(picked, axis=0, keepdims=True)
            root = jnp.sqrt(jnp.abs(gradient)) * GRAD_SCALE
            out_ref[at : at + 1, :] = jnp.where(gradient < 0.0, -root, root)


def grad(masked, losvd, occ, ids, message, after):
    hbm = pl.BlockSpec(memory_space=pltpu.HBM)
    vmem = pl.BlockSpec(memory_space=pltpu.VMEM)
    fetched = max((4096 - HELD) // GRAD_CHUNK, 1)
    return pl.pallas_call(
        grad_kernel,
        name="grad",
        in_specs=[vmem, hbm, vmem, vmem, vmem, hbm],
        out_specs=vmem,
        out_shape=jax.ShapeDtypeStruct((32, LANES), jnp.float32),
        scratch_shapes=[
            pltpu.VMEM((TEMPL, 8 * VBINS), jnp.bfloat16),
            pltpu.VMEM((fetched, 8, VBINS, GRAD_CHUNK), jnp.bfloat16),
            pltpu.SemaphoreType.DMA((fetched,)),
        ],
        compiler_params=pltpu.CompilerParams(vmem_limit_bytes=16 << 20),
        cost_estimate=pl.CostEstimate(flops=1 << 30, bytes_accessed=5 << 20, transcendentals=0),
    )(masked, pltpu.with_memory_space_constraint(losvd, pltpu.HBM), occ, ids, message, pltpu.with_memory_space_constraint(after, pltpu.HBM))


def assemble_kernel(r0_ref, r1_ref, r2_ref, r3_ref, out_ref):
    k = whereabouts()
    pieces = [r0_ref[...], r1_ref[...], r2_ref[...], r3_ref[...]]
    for group in range(GROUPS):
        j = jnp.bitwise_xor(k, group)
        piece = jnp.where(
            j < 2, jnp.where(j == 0, pieces[0], pieces[1]), jnp.where(j == 2, pieces[2], pieces[3])
        )
        for s in range(2):
            for q in range(4):
                out_ref[2 * group + s : 2 * group + s + 1, 1024 * q : 1024 * q + 1024] = piece[
                    4 * s + q : 4 * s + q + 1, :
                ]


def assemble(pieces):
    vmem = pl.BlockSpec(memory_space=pltpu.VMEM)
    return pl.pallas_call(
        assemble_kernel,
        name="assemble",
        in_specs=[vmem] * 4,
        out_shape=jax.ShapeDtypeStruct((8, WAVE), jnp.float32),
        compiler_params=pltpu.CompilerParams(vmem_limit_bytes=4 << 20),
    )(*pieces)


def step(weights, losvd, occupancy, template_of, templates, observed, inv_sigma):
    exchange = functools.partial(lax.all_to_all, split_axis=0, concat_axis=0, tiled=True)
    same_spaxels = [[GROUPS * p + k for p in range(MEMBERS)] for k in range(GROUPS)]
    rows = losvd.transpose(1, 2, 0)
    occ = occupancy.T
    ids = template_of.reshape(32, LANES)
    now = weights.reshape(32, LANES)

    def from_group(array, j):
        return lax.ppermute(array, "orb", [(i, i ^ j) for i in range(32)])

    gathered = [templates] + [from_group(templates, j) for j in range(1, GROUPS)]
    mixed, masked = mix(rows, occ, ids, now)
    shares = exchange(mixed.astype(jnp.float16), "orb").astype(jnp.float32)
    mixture = jnp.sum(shares * shares, axis=0) * (1.0 / MIX_SCALE**2)
    spectra, wanted = model(mixture, gathered)
    sent = (spectra * SPECTRUM_SCALE).astype(jnp.float16)
    parts = exchange(sent, "orb", axis_index_groups=same_spaxels).astype(jnp.float32)
    spectrum = jnp.sum(parts, axis=0) * (1.0 / SPECTRUM_SCALE)
    response, part = respond(spectrum, observed, inv_sigma, wanted)
    message = exchange(response, "orb")
    residual = assemble([part] + [from_group(part, j) for j in range(1, GROUPS)])
    roots = grad(masked, rows, occ, ids, message, residual).astype(jnp.float16)
    sums = exchange(jnp.broadcast_to(roots, (16, 32, LANES)), "spx").astype(jnp.float32)
    moved = jnp.sum(sums * jnp.abs(sums), axis=0) * (1.0 / GRAD_SCALE**2)
    return jnp.maximum(now - step_size * moved, 0.0).reshape(weights.shape), residual


def solution(mesh):
    placed = (
        P("orb"),
        P("orb", "spx", None),
        P("orb", "spx"),
        P("orb"),
        P("orb", None),
        P("spx", None),
        P("spx", None),
    )
    return jax.shard_map(step, mesh=mesh, in_specs=placed, out_specs=(P("orb"), P("spx", None)), check_vma=False)
```

```python
import functools

import jax
import jax.numpy as jnp
from jax import lax
from jax.experimental import pallas as pl
from jax.experimental.pallas import tpu as pltpu
from jax.sharding import PartitionSpec as P


step_size = 0.5

GROUPS = 4
MEMBERS = 8
LANES = 128
VBINS = 64
WAVE = 4096
TWAVE = 4160
WIDE = 4224
TEMPL = 256
PAIR = 128
MIX_CHUNK = 1024
HELD = 2048
GRAD_CHUNK = 1024
MIX_SCALE = 8192.0
GRAD_SCALE = 16.0
SPECTRUM_SCALE = 16.0


def masked_rows(rows, mask):
    parts = [rows[s] * jnp.broadcast_to(mask[s : s + 1, :], rows.shape[1:]) for s in range(8)]
    return jnp.concatenate(parts, axis=0)


def mask_of(occ, first, count):
    block = lax.broadcasted_iota(jnp.int32, (occ.shape[1], count), 0)
    orbit = lax.broadcasted_iota(jnp.int32, (occ.shape[1], count), 1)
    spread = (block == (first + orbit) // LANES).astype(jnp.bfloat16)
    return jnp.dot(
        occ.astype(jnp.bfloat16), spread, preferred_element_type=jnp.float32
    ).astype(jnp.bfloat16)


def mix_kernel(
    losvd_ref, occ_ref, ids_ref, weights_ref, out_ref, masked_ref, rows_ref, occ_buf, ids_buf, weights_buf, acc_ref, sems
):
    copies = [
        pltpu.make_async_copy(occ_ref, occ_buf, sems.at[0]),
        pltpu.make_async_copy(ids_ref, ids_buf, sems.at[1]),
        pltpu.make_async_copy(weights_ref, weights_buf, sems.at[2]),
    ]
    chunks = 4096 // MIX_CHUNK
    for c in range(chunks):
        source = losvd_ref.at[:, :, pl.ds(MIX_CHUNK * c, MIX_CHUNK)]
        copies.append(pltpu.make_async_copy(source, rows_ref.at[c], sems.at[3 + c]))
    for copy in copies:
        copy.start()
    for copy in copies[:3]:
        copy.wait()
    row = lax.broadcasted_iota(jnp.int32, (TEMPL, LANES), 0)
    blocks = MIX_CHUNK // LANES
    for c in range(chunks):
        parts = []
        for b in range(blocks * c, blocks * (c + 1)):
            ids = ids_buf[b : b + 1, :]
            wide = weights_buf[b : b + 1, :].astype(jnp.bfloat16).astype(jnp.float32)
            parts.append(jnp.where(row == ids, wide, 0.0).astype(jnp.bfloat16))
        assign = jnp.concatenate(parts, axis=1)
        mask = mask_of(occ_buf[...], MIX_CHUNK * c, MIX_CHUNK)
        copies[3 + c].wait()
        masked = masked_rows(rows_ref[c], mask)
        if MIX_CHUNK * c < HELD:
            masked_ref[:, MIX_CHUNK * c : MIX_CHUNK * (c + 1)] = masked
        part = lax.dot_general(
            assign, masked, (((1,), (1,)), ((), ())), preferred_element_type=jnp.float32
        )
        if c == 0:
            acc_ref[...] = part
        elif c < chunks - 1:
            acc_ref[...] += part
        else:
            acc_ref[...] = jnp.sqrt(acc_ref[...] + part) * MIX_SCALE
    for k in range(GROUPS):
        for p in range(MEMBERS):
            out_ref[GROUPS * p + k] = acc_ref[32 * p : 32 * p + 32, PAIR * k : PAIR * k + PAIR]


def mix(losvd, occ, ids, weights):
    hbm = pl.BlockSpec(memory_space=pltpu.HBM)
    vmem = pl.BlockSpec(memory_space=pltpu.VMEM)
    chunks = 4096 // MIX_CHUNK
    return pl.pallas_call(
        mix_kernel,
        name="mix",
        in_specs=[hbm] * 4,
        out_specs=[vmem, vmem],
        out_shape=[
            jax.ShapeDtypeStruct((32, 32, PAIR), jnp.float32),
            jax.ShapeDtypeStruct((8 * VBINS, HELD), jnp.bfloat16),
        ],
        scratch_shapes=[
            pltpu.VMEM((chunks, 8, VBINS, MIX_CHUNK), jnp.bfloat16),
            pltpu.VMEM((8, 32), jnp.int32),
            pltpu.VMEM((32, LANES), jnp.int32),
            pltpu.VMEM((32, LANES), jnp.float32),
            pltpu.VMEM((TEMPL, 8 * VBINS), jnp.float32),
            pltpu.SemaphoreType.DMA((3 + chunks,)),
        ],
        compiler_params=pltpu.CompilerParams(vmem_limit_bytes=16 << 20),
        cost_estimate=pl.CostEstimate(flops=1 << 30, bytes_accessed=5 << 20, transcendentals=0),
    )(*(pltpu.with_memory_space_constraint(x, pltpu.HBM) for x in (losvd, occ, ids, weights)))


def three_terms(x):
    high = x.astype(jnp.bfloat16)
    rest = x - high.astype(jnp.float32)
    middle = rest.astype(jnp.bfloat16)
    low = (rest - middle.astype(jnp.float32)).astype(jnp.bfloat16)
    return jnp.concatenate([high, middle, low], axis=0)


def whereabouts():
    index = lax.axis_index("orb")
    return lax.rem(index, GROUPS)


def own_order(k):
    return [pl.multiple_of(8 * jnp.bitwise_xor(k, j), 8) for j in range(GROUPS)]


def model_kernel(mixture_ref, t0_ref, t1_ref, t2_ref, t3_ref, out_ref, all_ref, wide_ref):
    mixture = jnp.concatenate([mixture_ref[pl.ds(at, 8), :] for at in own_order(whereabouts())], axis=0)
    terms = three_terms(mixture)
    templates = jnp.concatenate([t0_ref[...], t1_ref[...], t2_ref[...], t3_ref[...]], axis=0)
    all_ref[...] = templates
    tripled = jnp.concatenate([templates, templates, templates], axis=0)
    over_templates = (((0,), (0,)), ((), ()))
    wide_ref[:, :WAVE] = lax.dot_general(
        terms, tripled[:, :WAVE], over_templates, preferred_element_type=jnp.float32
    )
    wide_ref[:, WAVE:TWAVE] = lax.dot_general(
        terms, tripled[:, WAVE:], over_templates, preferred_element_type=jnp.float32
    )
    for s in range(2):
        rows = wide_ref[VBINS * s : VBINS * s + VBINS, :]
        for half in (32, 16, 8):
            rows = rows[:half] + pltpu.roll(rows[half : 2 * half], WIDE - half, 1)
        for half in (4, 2, 1):
            rows = rows + pltpu.roll(pltpu.roll(rows, 8 - half, 0), WIDE - half, 1)
        for q in range(4):
            piece = rows[0:1, 1024 * q : 1024 * q + 1024]
            for member in range(MEMBERS):
                out_ref[member, 4 * s + q : 4 * s + q + 1, :] = piece


def model(mixture, templates):
    vmem = pl.BlockSpec(memory_space=pltpu.VMEM)
    return pl.pallas_call(
        model_kernel,
        name="model",
        in_specs=[vmem] * 5,
        out_shape=[
            jax.ShapeDtypeStruct((MEMBERS, 8, 1024), jnp.float32),
            jax.ShapeDtypeStruct((32, TWAVE), jnp.bfloat16),
        ],
        scratch_shapes=[pltpu.VMEM((PAIR, WIDE), jnp.float32)],
        compiler_params=pltpu.CompilerParams(vmem_limit_bytes=24 << 20),
        cost_estimate=pl.CostEstimate(flops=1 << 27, bytes_accessed=1 << 20, transcendentals=0),
    )(mixture, *templates)


def respond_kernel(parts_ref, observed_ref, sigma_ref, templates_ref, out_ref, res_ref, shift_ref, rows_ref):
    k = whereabouts()
    total = parts_ref[...]
    templates = templates_ref[...]
    for s in range(2):
        spectrum = jnp.concatenate([total[4 * s + q : 4 * s + q + 1, :] for q in range(4)], axis=1)
        inverse = sigma_ref[pl.ds(2 * k + s, 1), :]
        residual = (spectrum - observed_ref[pl.ds(2 * k + s, 1), :]) * inverse
        for q in range(4):
            res_ref[4 * s + q : 4 * s + q + 1, :] = residual[:, 1024 * q : 1024 * q + 1024]
        scaled = (residual * inverse).astype(jnp.bfloat16).astype(jnp.float32)
        padded = jnp.concatenate([scaled, jnp.zeros((1, WIDE - WAVE), jnp.float32)], axis=1)
        spread = jnp.broadcast_to(padded, (VBINS, WIDE))
        shift_ref[VBINS * s : VBINS * s + VBINS, :] = pltpu.roll(
            spread, 0, 1, stride=1, stride_axis=0
        ).astype(jnp.bfloat16)
    over_waves = (((1,), (1,)), ((), ()))
    response = lax.dot_general(
        templates[:, :WAVE], shift_ref[:, :WAVE], over_waves, preferred_element_type=jnp.float32
    )
    response = response + lax.dot_general(
        templates[:, WAVE:], shift_ref[:, WAVE:TWAVE], over_waves, preferred_element_type=jnp.float32
    )
    for j, at in enumerate(own_order(k)):
        rows_ref[pl.ds(at, 8), :] = response[8 * j : 8 * j + 8]
    message = rows_ref[...].astype(jnp.bfloat16)
    for target in range(32):
        out_ref[target] = message


def respond(parts, observed, sigma, templates):
    vmem = pl.BlockSpec(memory_space=pltpu.VMEM)
    return pl.pallas_call(
        respond_kernel,
        name="respond",
        in_specs=[vmem] * 4,
        out_shape=[
            jax.ShapeDtypeStruct((32, 32, PAIR), jnp.bfloat16),
            jax.ShapeDtypeStruct((8, 1024), jnp.float32),
        ],
        scratch_shapes=[
            pltpu.VMEM((PAIR, WIDE), jnp.bfloat16),
            pltpu.VMEM((32, PAIR), jnp.float32),
        ],
        compiler_params=pltpu.CompilerParams(vmem_limit_bytes=24 << 20),
        cost_estimate=pl.CostEstimate(flops=1 << 27, bytes_accessed=1 << 20, transcendentals=0),
    )(parts, observed, sigma, templates)


def grad_kernel(
    masked_ref, losvd_ref, occ_ref, ids_ref, message_ref, out_ref, table_ref, rows_ref, sems
):
    chunks = 4096 // GRAD_CHUNK
    held = HELD // GRAD_CHUNK
    copies = []
    for c in range(held, chunks):
        source = losvd_ref.at[:, :, pl.ds(GRAD_CHUNK * c, GRAD_CHUNK)]
        copies.append(pltpu.make_async_copy(source, rows_ref.at[c - held], sems.at[c - held]))
    for copy in copies:
        copy.start()
    for k in range(GROUPS):
        for p in range(MEMBERS):
            table_ref[32 * p : 32 * p + 32, PAIR * k : PAIR * k + PAIR] = message_ref[GROUPS * p + k]
    row = lax.broadcasted_iota(jnp.int32, (TEMPL, LANES), 0)
    for c in range(chunks):
        if c < held:
            masked = masked_ref[:, GRAD_CHUNK * c : GRAD_CHUNK * (c + 1)]
        else:
            mask = mask_of(occ_ref[...], GRAD_CHUNK * c, GRAD_CHUNK)
            copies[c - held].wait()
            masked = masked_rows(rows_ref[c - held], mask)
        scores = jnp.dot(table_ref[...], masked, preferred_element_type=jnp.float32)
        for b in range(GRAD_CHUNK // LANES):
            at = GRAD_CHUNK // LANES * c + b
            ids = ids_ref[at : at + 1, :]
            picked = jnp.where(row == ids, scores[:, LANES * b : LANES * b + LANES], 0.0)
            gradient = jnp.sum(picked, axis=0, keepdims=True)
            root = jnp.sqrt(jnp.abs(gradient)) * GRAD_SCALE
            out_ref[at : at + 1, :] = jnp.where(gradient < 0.0, -root, root)


def grad(masked, losvd, occ, ids, message):
    hbm = pl.BlockSpec(memory_space=pltpu.HBM)
    vmem = pl.BlockSpec(memory_space=pltpu.VMEM)
    fetched = max((4096 - HELD) // GRAD_CHUNK, 1)
    return pl.pallas_call(
        grad_kernel,
        name="grad",
        in_specs=[vmem, hbm, vmem, vmem, vmem],
        out_specs=vmem,
        out_shape=jax.ShapeDtypeStruct((32, LANES), jnp.float32),
        scratch_shapes=[
            pltpu.VMEM((TEMPL, 8 * VBINS), jnp.bfloat16),
            pltpu.VMEM((fetched, 8, VBINS, GRAD_CHUNK), jnp.bfloat16),
            pltpu.SemaphoreType.DMA((fetched,)),
        ],
        compiler_params=pltpu.CompilerParams(vmem_limit_bytes=16 << 20),
        cost_estimate=pl.CostEstimate(flops=1 << 30, bytes_accessed=5 << 20, transcendentals=0),
    )(masked, pltpu.with_memory_space_constraint(losvd, pltpu.HBM), occ, ids, message)


def finish_kernel(weights_ref, moved_ref, r0_ref, r1_ref, r2_ref, r3_ref, next_ref, out_ref):
    next_ref[...] = jnp.maximum(weights_ref[...] - step_size * moved_ref[...], 0.0)
    k = whereabouts()
    pieces = [r0_ref[...], r1_ref[...], r2_ref[...], r3_ref[...]]
    for group in range(GROUPS):
        j = jnp.bitwise_xor(k, group)
        piece = jnp.where(
            j < 2, jnp.where(j == 0, pieces[0], pieces[1]), jnp.where(j == 2, pieces[2], pieces[3])
        )
        for s in range(2):
            for q in range(4):
                out_ref[2 * group + s : 2 * group + s + 1, 1024 * q : 1024 * q + 1024] = piece[
                    4 * s + q : 4 * s + q + 1, :
                ]


def finish(weights, moved, pieces):
    vmem = pl.BlockSpec(memory_space=pltpu.VMEM)
    return pl.pallas_call(
        finish_kernel,
        name="finish",
        in_specs=[vmem] * 6,
        out_shape=[
            jax.ShapeDtypeStruct((32, LANES), jnp.float32),
            jax.ShapeDtypeStruct((8, WAVE), jnp.float32),
        ],
        compiler_params=pltpu.CompilerParams(vmem_limit_bytes=4 << 20),
    )(weights, moved, *pieces)


def step(weights, losvd, occupancy, template_of, templates, observed, inv_sigma):
    exchange = functools.partial(lax.all_to_all, split_axis=0, concat_axis=0, tiled=True)
    same_spaxels = [[GROUPS * p + k for p in range(MEMBERS)] for k in range(GROUPS)]
    rows = losvd.transpose(1, 2, 0)
    occ = occupancy.T
    ids = template_of.reshape(32, LANES)
    now = weights.reshape(32, LANES)

    def from_group(array, j):
        return lax.ppermute(array, "orb", [(i, i ^ j) for i in range(32)])

    gathered = [templates] + [from_group(templates, j) for j in range(1, GROUPS)]
    mixed, masked = mix(rows, occ, ids, now)
    shares = exchange(mixed.astype(jnp.float16), "orb").astype(jnp.float32)
    mixture = jnp.sum(shares * shares, axis=0) * (1.0 / MIX_SCALE**2)
    spectra, wanted = model(mixture, gathered)
    sent = (spectra * SPECTRUM_SCALE).astype(jnp.float16)
    parts = exchange(sent, "orb", axis_index_groups=same_spaxels).astype(jnp.float32)
    spectrum = jnp.sum(parts, axis=0) * (1.0 / SPECTRUM_SCALE)
    response, part = respond(spectrum, observed, inv_sigma, wanted)
    message = exchange(response, "orb")
    pieces = [part] + [from_group(part, j) for j in range(1, GROUPS)]
    roots = grad(masked, rows, occ, ids, message).astype(jnp.float16)
    sums = exchange(jnp.broadcast_to(roots, (16, 32, LANES)), "spx").astype(jnp.float32)
    moved = jnp.sum(sums * jnp.abs(sums), axis=0) * (1.0 / GRAD_SCALE**2)
    after, residual = finish(now, moved, pieces)
    return after.reshape(weights.shape), residual


def solution(mesh):
    placed = (
        P("orb"),
        P("orb", "spx", None),
        P("orb", "spx"),
        P("orb"),
        P("orb", None),
        P("spx", None),
        P("spx", None),
    )
    return jax.shard_map(
        step, mesh=mesh, in_specs=placed, out_specs=(P("orb"), P("spx", None)), check_vma=False
    )
```

```python
import functools

import jax
import jax.numpy as jnp
from jax import lax
from jax.experimental import pallas as pl
from jax.experimental.pallas import tpu as pltpu
from jax.sharding import PartitionSpec as P


step_size = 0.5

GROUPS = 4
MEMBERS = 8
LANES = 128
VBINS = 64
WAVE = 4096
TWAVE = 4160
WIDE = 4224
TEMPL = 256
PAIR = 128
MIX_CHUNK = 1024
HELD = 3072
GRAD_CHUNK = 1024
MIX_SCALE = 8192.0
GRAD_SCALE = 16.0
SPECTRUM_SCALE = 16.0


def masked_rows(rows, mask):
    parts = [rows[s] * jnp.broadcast_to(mask[s : s + 1, :], rows.shape[1:]) for s in range(8)]
    return jnp.concatenate(parts, axis=0)


def mask_of(occ, first, count):
    block = lax.broadcasted_iota(jnp.int32, (occ.shape[1], count), 0)
    orbit = lax.broadcasted_iota(jnp.int32, (occ.shape[1], count), 1)
    spread = (block == (first + orbit) // LANES).astype(jnp.bfloat16)
    return jnp.dot(
        occ.astype(jnp.bfloat16), spread, preferred_element_type=jnp.float32
    ).astype(jnp.bfloat16)


def mix_kernel(
    losvd_ref, occ_ref, ids_ref, weights_ref, out_ref, masked_ref, rows_ref, occ_buf, ids_buf, weights_buf, acc_ref, sems
):
    copies = [
        pltpu.make_async_copy(occ_ref, occ_buf, sems.at[0]),
        pltpu.make_async_copy(ids_ref, ids_buf, sems.at[1]),
        pltpu.make_async_copy(weights_ref, weights_buf, sems.at[2]),
    ]
    chunks = 4096 // MIX_CHUNK
    for c in range(chunks):
        source = losvd_ref.at[:, :, pl.ds(MIX_CHUNK * c, MIX_CHUNK)]
        copies.append(pltpu.make_async_copy(source, rows_ref.at[c], sems.at[3 + c]))
    for copy in copies:
        copy.start()
    for copy in copies[:3]:
        copy.wait()
    row = lax.broadcasted_iota(jnp.int32, (TEMPL, LANES), 0)
    blocks = MIX_CHUNK // LANES
    for c in range(chunks):
        parts = []
        for b in range(blocks * c, blocks * (c + 1)):
            ids = ids_buf[b : b + 1, :]
            wide = weights_buf[b : b + 1, :].astype(jnp.bfloat16).astype(jnp.float32)
            parts.append(jnp.where(row == ids, wide, 0.0).astype(jnp.bfloat16))
        assign = jnp.concatenate(parts, axis=1)
        mask = mask_of(occ_buf[...], MIX_CHUNK * c, MIX_CHUNK)
        copies[3 + c].wait()
        masked = masked_rows(rows_ref[c], mask)
        if MIX_CHUNK * c < HELD:
            masked_ref[:, MIX_CHUNK * c : MIX_CHUNK * (c + 1)] = masked
        part = lax.dot_general(
            assign, masked, (((1,), (1,)), ((), ())), preferred_element_type=jnp.float32
        )
        if c == 0:
            acc_ref[...] = part
        elif c < chunks - 1:
            acc_ref[...] += part
        else:
            acc_ref[...] = jnp.sqrt(acc_ref[...] + part) * MIX_SCALE
    for k in range(GROUPS):
        for p in range(MEMBERS):
            out_ref[GROUPS * p + k] = acc_ref[32 * p : 32 * p + 32, PAIR * k : PAIR * k + PAIR]


def mix(losvd, occ, ids, weights):
    hbm = pl.BlockSpec(memory_space=pltpu.HBM)
    vmem = pl.BlockSpec(memory_space=pltpu.VMEM)
    chunks = 4096 // MIX_CHUNK
    return pl.pallas_call(
        mix_kernel,
        name="mix",
        in_specs=[hbm] * 4,
        out_specs=[vmem, vmem],
        out_shape=[
            jax.ShapeDtypeStruct((32, 32, PAIR), jnp.float32),
            jax.ShapeDtypeStruct((8 * VBINS, HELD), jnp.bfloat16),
        ],
        scratch_shapes=[
            pltpu.VMEM((chunks, 8, VBINS, MIX_CHUNK), jnp.bfloat16),
            pltpu.VMEM((8, 32), jnp.int32),
            pltpu.VMEM((32, LANES), jnp.int32),
            pltpu.VMEM((32, LANES), jnp.float32),
            pltpu.VMEM((TEMPL, 8 * VBINS), jnp.float32),
            pltpu.SemaphoreType.DMA((3 + chunks,)),
        ],
        compiler_params=pltpu.CompilerParams(vmem_limit_bytes=16 << 20),
        cost_estimate=pl.CostEstimate(flops=1 << 30, bytes_accessed=5 << 20, transcendentals=0),
    )(*(pltpu.with_memory_space_constraint(x, pltpu.HBM) for x in (losvd, occ, ids, weights)))


def three_terms(x):
    high = x.astype(jnp.bfloat16)
    rest = x - high.astype(jnp.float32)
    middle = rest.astype(jnp.bfloat16)
    low = (rest - middle.astype(jnp.float32)).astype(jnp.bfloat16)
    return jnp.concatenate([high, middle, low], axis=0)


def whereabouts():
    index = lax.axis_index("orb")
    return lax.rem(index, GROUPS)


def own_order(k):
    return [pl.multiple_of(8 * jnp.bitwise_xor(k, j), 8) for j in range(GROUPS)]


def model_kernel(mixture_ref, t0_ref, t1_ref, t2_ref, t3_ref, out_ref, all_ref, wide_ref):
    mixture = jnp.concatenate([mixture_ref[pl.ds(at, 8), :] for at in own_order(whereabouts())], axis=0)
    terms = three_terms(mixture)
    templates = jnp.concatenate([t0_ref[...], t1_ref[...], t2_ref[...], t3_ref[...]], axis=0)
    all_ref[...] = templates
    tripled = jnp.concatenate([templates, templates, templates], axis=0)
    over_templates = (((0,), (0,)), ((), ()))
    wide_ref[:, :WAVE] = lax.dot_general(
        terms, tripled[:, :WAVE], over_templates, preferred_element_type=jnp.float32
    )
    wide_ref[:, WAVE:TWAVE] = lax.dot_general(
        terms, tripled[:, WAVE:], over_templates, preferred_element_type=jnp.float32
    )
    for s in range(2):
        rows = wide_ref[VBINS * s : VBINS * s + VBINS, :]
        for half in (32, 16, 8):
            rows = rows[:half] + pltpu.roll(rows[half : 2 * half], WIDE - half, 1)
        for half in (4, 2, 1):
            rows = rows + pltpu.roll(pltpu.roll(rows, 8 - half, 0), WIDE - half, 1)
        for q in range(4):
            piece = rows[0:1, 1024 * q : 1024 * q + 1024]
            for member in range(MEMBERS):
                out_ref[member, 4 * s + q : 4 * s + q + 1, :] = piece


def model(mixture, templates):
    vmem = pl.BlockSpec(memory_space=pltpu.VMEM)
    return pl.pallas_call(
        model_kernel,
        name="model",
        in_specs=[vmem] * 5,
        out_shape=[
            jax.ShapeDtypeStruct((MEMBERS, 8, 1024), jnp.float32),
            jax.ShapeDtypeStruct((32, TWAVE), jnp.bfloat16),
        ],
        scratch_shapes=[pltpu.VMEM((PAIR, WIDE), jnp.float32)],
        compiler_params=pltpu.CompilerParams(vmem_limit_bytes=24 << 20),
        cost_estimate=pl.CostEstimate(flops=1 << 27, bytes_accessed=1 << 20, transcendentals=0),
    )(mixture, *templates)


def respond_kernel(parts_ref, observed_ref, sigma_ref, templates_ref, out_ref, res_ref, shift_ref, rows_ref):
    k = whereabouts()
    total = parts_ref[...]
    templates = templates_ref[...]
    for s in range(2):
        spectrum = jnp.concatenate([total[4 * s + q : 4 * s + q + 1, :] for q in range(4)], axis=1)
        inverse = sigma_ref[pl.ds(2 * k + s, 1), :]
        residual = (spectrum - observed_ref[pl.ds(2 * k + s, 1), :]) * inverse
        for q in range(4):
            res_ref[4 * s + q : 4 * s + q + 1, :] = residual[:, 1024 * q : 1024 * q + 1024]
        scaled = (residual * inverse).astype(jnp.bfloat16).astype(jnp.float32)
        padded = jnp.concatenate([scaled, jnp.zeros((1, WIDE - WAVE), jnp.float32)], axis=1)
        spread = jnp.broadcast_to(padded, (VBINS, WIDE))
        shift_ref[VBINS * s : VBINS * s + VBINS, :] = pltpu.roll(
            spread, 0, 1, stride=1, stride_axis=0
        ).astype(jnp.bfloat16)
    over_waves = (((1,), (1,)), ((), ()))
    response = lax.dot_general(
        templates[:, :WAVE], shift_ref[:, :WAVE], over_waves, preferred_element_type=jnp.float32
    )
    response = response + lax.dot_general(
        templates[:, WAVE:], shift_ref[:, WAVE:TWAVE], over_waves, preferred_element_type=jnp.float32
    )
    for j, at in enumerate(own_order(k)):
        rows_ref[pl.ds(at, 8), :] = response[8 * j : 8 * j + 8]
    message = rows_ref[...].astype(jnp.bfloat16)
    for target in range(32):
        out_ref[target] = message


def respond(parts, observed, sigma, templates):
    vmem = pl.BlockSpec(memory_space=pltpu.VMEM)
    return pl.pallas_call(
        respond_kernel,
        name="respond",
        in_specs=[vmem] * 4,
        out_shape=[
            jax.ShapeDtypeStruct((32, 32, PAIR), jnp.bfloat16),
            jax.ShapeDtypeStruct((8, 1024), jnp.float32),
        ],
        scratch_shapes=[
            pltpu.VMEM((PAIR, WIDE), jnp.bfloat16),
            pltpu.VMEM((32, PAIR), jnp.float32),
        ],
        compiler_params=pltpu.CompilerParams(vmem_limit_bytes=24 << 20),
        cost_estimate=pl.CostEstimate(flops=1 << 27, bytes_accessed=1 << 20, transcendentals=0),
    )(parts, observed, sigma, templates)


def grad_kernel(
    masked_ref, losvd_ref, occ_ref, ids_ref, message_ref, out_ref, table_ref, rows_ref, sems
):
    chunks = 4096 // GRAD_CHUNK
    held = HELD // GRAD_CHUNK
    copies = []
    for c in range(held, chunks):
        source = losvd_ref.at[:, :, pl.ds(GRAD_CHUNK * c, GRAD_CHUNK)]
        copies.append(pltpu.make_async_copy(source, rows_ref.at[c - held], sems.at[c - held]))
    for copy in copies:
        copy.start()
    for k in range(GROUPS):
        for p in range(MEMBERS):
            table_ref[32 * p : 32 * p + 32, PAIR * k : PAIR * k + PAIR] = message_ref[GROUPS * p + k]
    row = lax.broadcasted_iota(jnp.int32, (TEMPL, LANES), 0)
    for c in range(chunks):
        if c < held:
            masked = masked_ref[:, GRAD_CHUNK * c : GRAD_CHUNK * (c + 1)]
        else:
            mask = mask_of(occ_ref[...], GRAD_CHUNK * c, GRAD_CHUNK)
            copies[c - held].wait()
            masked = masked_rows(rows_ref[c - held], mask)
        scores = jnp.dot(table_ref[...], masked, preferred_element_type=jnp.float32)
        for b in range(GRAD_CHUNK // LANES):
            at = GRAD_CHUNK // LANES * c + b
            ids = ids_ref[at : at + 1, :]
            picked = jnp.where(row == ids, scores[:, LANES * b : LANES * b + LANES], 0.0)
            gradient = jnp.sum(picked, axis=0, keepdims=True)
            root = jnp.sqrt(jnp.abs(gradient)) * GRAD_SCALE
            out_ref[at : at + 1, :] = jnp.where(gradient < 0.0, -root, root)


def grad(masked, losvd, occ, ids, message):
    hbm = pl.BlockSpec(memory_space=pltpu.HBM)
    vmem = pl.BlockSpec(memory_space=pltpu.VMEM)
    fetched = max((4096 - HELD) // GRAD_CHUNK, 1)
    return pl.pallas_call(
        grad_kernel,
        name="grad",
        in_specs=[vmem, hbm, vmem, vmem, vmem],
        out_specs=vmem,
        out_shape=jax.ShapeDtypeStruct((32, LANES), jnp.float32),
        scratch_shapes=[
            pltpu.VMEM((TEMPL, 8 * VBINS), jnp.bfloat16),
            pltpu.VMEM((fetched, 8, VBINS, GRAD_CHUNK), jnp.bfloat16),
            pltpu.SemaphoreType.DMA((fetched,)),
        ],
        compiler_params=pltpu.CompilerParams(vmem_limit_bytes=16 << 20),
        cost_estimate=pl.CostEstimate(flops=1 << 30, bytes_accessed=5 << 20, transcendentals=0),
    )(masked, pltpu.with_memory_space_constraint(losvd, pltpu.HBM), occ, ids, message)


def finish_kernel(weights_ref, moved_ref, r0_ref, r1_ref, r2_ref, r3_ref, next_ref, out_ref):
    next_ref[...] = jnp.maximum(weights_ref[...] - step_size * moved_ref[...], 0.0)
    k = whereabouts()
    pieces = [r0_ref[...], r1_ref[...], r2_ref[...], r3_ref[...]]
    for group in range(GROUPS):
        j = jnp.bitwise_xor(k, group)
        piece = jnp.where(
            j < 2, jnp.where(j == 0, pieces[0], pieces[1]), jnp.where(j == 2, pieces[2], pieces[3])
        )
        for s in range(2):
            for q in range(4):
                out_ref[2 * group + s : 2 * group + s + 1, 1024 * q : 1024 * q + 1024] = piece[
                    4 * s + q : 4 * s + q + 1, :
                ]


def finish(weights, moved, pieces):
    vmem = pl.BlockSpec(memory_space=pltpu.VMEM)
    return pl.pallas_call(
        finish_kernel,
        name="finish",
        in_specs=[vmem] * 6,
        out_shape=[
            jax.ShapeDtypeStruct((32, LANES), jnp.float32),
            jax.ShapeDtypeStruct((8, WAVE), jnp.float32),
        ],
        compiler_params=pltpu.CompilerParams(vmem_limit_bytes=4 << 20),
    )(weights, moved, *pieces)


def step(weights, losvd, occupancy, template_of, templates, observed, inv_sigma):
    exchange = functools.partial(lax.all_to_all, split_axis=0, concat_axis=0, tiled=True)
    same_spaxels = [[GROUPS * p + k for p in range(MEMBERS)] for k in range(GROUPS)]
    rows = losvd.transpose(1, 2, 0)
    occ = occupancy.T
    ids = template_of.reshape(32, LANES)
    now = weights.reshape(32, LANES)

    def from_group(array, j):
        return lax.ppermute(array, "orb", [(i, i ^ j) for i in range(32)])

    gathered = [templates]
    for j in range(1, GROUPS):
        gathered.append(from_group(templates, j))
    mixed, masked = mix(rows, occ, ids, now)
    shares = exchange(mixed.astype(jnp.float16), "orb").astype(jnp.float32)
    mixture = jnp.sum(shares * shares, axis=0) * (1.0 / MIX_SCALE**2)
    spectra, wanted = model(mixture, gathered)
    sent = (spectra * SPECTRUM_SCALE).astype(jnp.float16)
    parts = exchange(sent, "orb", axis_index_groups=same_spaxels).astype(jnp.float32)
    spectrum = jnp.sum(parts, axis=0) * (1.0 / SPECTRUM_SCALE)
    response, part = respond(spectrum, observed, inv_sigma, wanted)
    message = exchange(response, "orb")
    pieces = [part] + [from_group(part, j) for j in range(1, GROUPS)]
    roots = grad(masked, rows, occ, ids, message).astype(jnp.float16)
    sums = exchange(jnp.broadcast_to(roots, (16, 32, LANES)), "spx").astype(jnp.float32)
    moved = jnp.sum(sums * jnp.abs(sums), axis=0) * (1.0 / GRAD_SCALE**2)
    after, residual = finish(now, moved, pieces)
    return after.reshape(weights.shape), residual


def solution(mesh):
    placed = (
        P("orb"),
        P("orb", "spx", None),
        P("orb", "spx"),
        P("orb"),
        P("orb", None),
        P("spx", None),
        P("spx", None),
    )
    return jax.shard_map(
        step, mesh=mesh, in_specs=placed, out_specs=(P("orb"), P("spx", None)), check_vma=False
    )
```
